32 devices in a mesh: sec: 2 (over core), blk: 8 (over z, x), ch: 2 (over y).
Axes of the slice: x: 2, y: 2, z: 4, core: 2. Of those that a mesh axis runs over, the one named last changes fastest.
Arguments:
- voltages: bfloat16 [123, 4096, 2048], P(None, 'blk', ('sec', 'ch')), may hold values from -6 to 6
Outputs:
- visibilities: bfloat16 [16, 2, 4096, 4096], P(('sec', 'ch'), None, 'blk')
The draws below stay inside these ranges and needn't reach their ends.
All inputs are finite; a program needn't handle non-finite values.
Results may differ from the reference program's by a relative error of at most 0.0082.
Values may be sent and summed in bfloat16 or wider, within the bound.
A program may use at most 384 MiB of HBM per device.

```python
import math
import jax
import jax.numpy as jnp
from jax import lax

STREAMS = 4096
FFT = 2048
TAPS = 4
TIME = 120
NCHAN = 1024
CHAN = 16
FRAMES = 123
PANEL = 512
N_BLK = 8


def steps_of(key, extent, shards, least, high):
    def one(dim, blocks):
        draws = jax.random.uniform(jax.random.fold_in(jax.random.fold_in(key, 6), dim), (blocks,), jnp.float32, least / len(shards), high / len(shards))
        return jnp.repeat(jnp.exp(draws), extent[dim] // blocks).reshape((-1,) + (1,) * (len(extent) - dim - 1))

    factor_of = one(*shards[0])
    for cut in shards[1:]:
        factor_of = factor_of * one(*cut)
    return factor_of


def bell_draw(rng, dims, width, most, shards=(), kind=jnp.bfloat16):
    entries = jax.random.normal(rng, dims, jnp.float32) * width
    if len(shards) > 0:
        entries = steps_of(rng, dims, shards, -0.22, 0.18) * entries
    return jnp.clip(entries, min=-most, max=most).astype(kind)


def setup_inputs(seed: int = 0) -> dict:
    seeds = jax.random.split(jax.random.key(seed), 2)
    return {
        "voltages": bell_draw(seeds[0], (FRAMES, STREAMS, FFT), 1.0, 6.0, ((1, 8), (2, 4))),
    }


def make_window(tap_count, frame_len):
    position = jnp.arange(tap_count * frame_len, dtype=jnp.float32)
    offset = (position - tap_count * frame_len / 2 + 0.5) / frame_len
    taper = 0.5 - 0.5 * jnp.cos(2.0 * jnp.pi * (position + 0.5) / (tap_count * frame_len))
    profile = jnp.sinc(offset) * taper
    profile = profile * jnp.sqrt(frame_len / jnp.sum(profile * profile))
    return profile.reshape(tap_count, frame_len)

def dft_table(frame_len, chan_count, bank_size):
    spacing = bank_size // chan_count
    chosen = jnp.arange(chan_count, dtype=jnp.int32) * spacing + spacing // 2
    phases = jnp.arange(frame_len, dtype=jnp.int32)[:, None] * chosen[None, :] % frame_len
    angles = 2.0 * jnp.pi / frame_len * phases.astype(jnp.float32)
    factor = 1.0 / math.sqrt(frame_len)
    weights = jnp.stack([jnp.cos(angles) * factor, -jnp.sin(angles) * factor], axis=-1)
    return weights.reshape(frame_len, chan_count * 2).astype(jnp.bfloat16)

def reference(voltages):
    window = make_window(TAPS, FFT)
    weights = dft_table(FFT, CHAN, NCHAN)

    def channelise(group_index):
        inputs_block = lax.dynamic_slice_in_dim(voltages, group_index * PANEL, PANEL, 1)
        summed = jnp.zeros((TIME, PANEL, FFT), jnp.float32)
        for tap_index in range(TAPS):
            summed = summed + window[tap_index] * inputs_block[tap_index:tap_index + TIME].astype(jnp.float32)
        filtered = summed.astype(jnp.bfloat16)
        spectrum = jnp.dot(filtered.reshape(TIME * PANEL, FFT), weights, preferred_element_type=jnp.float32)
        return spectrum.astype(jnp.bfloat16).reshape(TIME, PANEL, CHAN, 2)
    pieces = lax.map(channelise, jnp.arange(N_BLK, dtype=jnp.int32))
    spectra = pieces.transpose(3, 4, 1, 0, 2).reshape(CHAN, 2, TIME, STREAMS)

    def correlate(chan_spectra):
        real_part = chan_spectra[0]
        imag_part = chan_spectra[1]
        real_sum = jnp.dot(real_part.T, real_part, preferred_element_type=jnp.float32) + jnp.dot(imag_part.T, imag_part, preferred_element_type=jnp.float32)
        imag_sum = jnp.dot(imag_part.T, real_part, preferred_element_type=jnp.float32) - jnp.dot(real_part.T, imag_part, preferred_element_type=jnp.float32)
        return (jnp.stack([real_sum, imag_sum]) / TIME).astype(jnp.bfloat16)
    return lax.map(correlate, spectra)
```

```python
import functools
import math

import jax
import jax.numpy as jnp
from jax import lax
from jax.experimental import pallas as pl
from jax.experimental.pallas import tpu as pltpu
from jax.sharding import PartitionSpec as P

FFT = 2048
TAPS = 4
CH_GRP = 4
LANES = 128


def make_window(tap_count, frame_len):
    position = jnp.arange(tap_count * frame_len, dtype=jnp.float32)
    offset = (position - tap_count * frame_len / 2 + 0.5) / frame_len
    taper = 0.5 - 0.5 * jnp.cos(2.0 * jnp.pi * (position + 0.5) / (tap_count * frame_len))
    profile = jnp.sinc(offset) * taper
    profile = profile * jnp.sqrt(frame_len / jnp.sum(profile * profile))
    return profile.reshape(tap_count, frame_len)


def dft_rows(first, span_len, frame_len, chan_count, bank_size):
    spacing = bank_size // chan_count
    row = jnp.arange(2 * chan_count, dtype=jnp.int32)
    chosen = row // 2 * spacing + spacing // 2
    sample = first + jnp.arange(span_len, dtype=jnp.int32)
    phases = chosen[:, None] * sample[None, :] % frame_len
    angles = 2.0 * jnp.pi / frame_len * phases.astype(jnp.float32)
    factor = 1.0 / math.sqrt(frame_len)
    wave = jnp.where(row[:, None] % 2 == 0, jnp.cos(angles), -jnp.sin(angles)) * factor
    return wave.astype(jnp.bfloat16).astype(jnp.float32)


def bank_kernel(steps, chunk, volts_ref, weights_ref, out_ref, products):
    part = pl.program_id(1)
    rows = weights_ref.shape[0] // TAPS
    weights = weights_ref[...]

    for frame in range(chunk):
        products[part * chunk + frame] = lax.dot_general(
            weights,
            volts_ref[frame],
            (((1,), (1,)), ((), ())),
            preferred_element_type=jnp.float32,
        )

    def add_taps(step, carry):
        total = products[step, 0:rows]
        for tap in range(1, TAPS):
            total = total + products[step + tap, tap * rows : (tap + 1) * rows]
        out_ref[pl.ds(step, rows, stride=steps), :] = total
        return carry

    low = jnp.maximum(part * chunk - (TAPS - 1), 0)
    lax.fori_loop(low, (part + 1) * chunk - (TAPS - 1), add_taps, 0)


def filter_bank(voltages, weights):
    frames, panel_len, span_len = voltages.shape
    steps = frames - TAPS + 1
    rows = weights.shape[0] // TAPS
    chunk = next(size for size in (41, 3, 1) if frames % size == 0)
    return pl.pallas_call(
        functools.partial(bank_kernel, steps, chunk),
        grid=(panel_len // LANES, frames // chunk),
        in_specs=[
            pl.BlockSpec((chunk, LANES, span_len), lambda s, f: (f, s, 0)),
            pl.BlockSpec(weights.shape, lambda s, f: (0, 0)),
        ],
        out_specs=pl.BlockSpec((rows * steps, LANES), lambda s, f: (0, s)),
        out_shape=jax.ShapeDtypeStruct((rows * steps, panel_len), jnp.float32),
        scratch_shapes=[pltpu.VMEM((frames, weights.shape[0], LANES), jnp.float32)],
        compiler_params=pltpu.CompilerParams(vmem_limit_bytes=48 * 1024 * 1024),
    )(voltages, weights)


def pair_kernel(steps, local_ref, remote_ref, out_ref, lhs):
    panel_len = local_ref.shape[2]

    @pl.when(pl.program_id(1) == 0)
    def _():
        turned = local_ref[0].astype(jnp.float32).T
        lhs[0:panel_len, :] = turned.astype(jnp.bfloat16)
        other = jnp.concatenate([turned[:, steps:], -turned[:, :steps]], axis=1)
        lhs[panel_len:, :] = other.astype(jnp.bfloat16)

    sums = jnp.dot(lhs[...], remote_ref[0, 0], preferred_element_type=jnp.float32)
    scaled = (sums * (1.0 / steps)).astype(jnp.bfloat16)
    out_ref[0, 0] = scaled[:panel_len]
    out_ref[0, 1] = scaled[panel_len:]


def correlate(local, gathered):
    chans, depth, panel_len = local.shape
    panels = gathered.shape[0]
    return pl.pallas_call(
        functools.partial(pair_kernel, depth // 2),
        grid=(chans, panels),
        in_specs=[
            pl.BlockSpec((1, depth, panel_len), lambda c, j: (c, 0, 0)),
            pl.BlockSpec((1, 1, depth, panel_len), lambda c, j: (j, c, 0, 0)),
        ],
        out_specs=pl.BlockSpec((1, 2, panel_len, panel_len), lambda c, j: (c, 0, 0, j)),
        out_shape=jax.ShapeDtypeStruct((chans, 2, panel_len, panels * panel_len), jnp.bfloat16),
        scratch_shapes=[pltpu.VMEM((2 * panel_len, depth), jnp.bfloat16)],
        compiler_params=pltpu.CompilerParams(vmem_limit_bytes=32 * 1024 * 1024),
    )(local, gathered)


def body(voltages):
    groups = lax.axis_size("sec") * lax.axis_size("ch")
    frames, panel_len, span_len = voltages.shape
    steps = frames - TAPS + 1
    chan_total = CH_GRP * groups
    group_pos = lax.axis_index("sec") * lax.axis_size("ch") + lax.axis_index("ch")
    first = group_pos * span_len
    window = lax.dynamic_slice_in_dim(make_window(TAPS, FFT), first, span_len, 1)
    table = dft_rows(first, span_len, FFT, chan_total, FFT // 2)
    weights = (window[:, None, :] * table[None]).astype(jnp.bfloat16)
    terms = filter_bank(voltages, weights.reshape(TAPS * 2 * chan_total, span_len))
    spectra = lax.psum_scatter(
        terms.reshape(chan_total, 2 * steps, panel_len),
        ("sec", "ch"),
        scatter_dimension=0,
        tiled=True,
    ).astype(jnp.bfloat16)
    return correlate(spectra, lax.all_gather(spectra, "blk", axis=0))


def solution(mesh):
    return jax.shard_map(
        body,
        mesh=mesh,
        in_specs=(P(None, "blk", ("sec", "ch")),),
        out_specs=P(("sec", "ch"), None, "blk", None),
        check_vma=False,
    )
```

```python
import functools
import math

import jax
import jax.numpy as jnp
from jax import lax
from jax.experimental import pallas as pl
from jax.experimental.pallas import tpu as pltpu
from jax.sharding import PartitionSpec as P

FFT = 2048
TAPS = 4
CH_GRP = 4
LANES = 128
MESH = pl.DeviceIdType.MESH


def make_window(tap_count, frame_len):
    position = jnp.arange(tap_count * frame_len, dtype=jnp.float32)
    offset = (position - tap_count * frame_len / 2 + 0.5) / frame_len
    taper = 0.5 - 0.5 * jnp.cos(2.0 * jnp.pi * (position + 0.5) / (tap_count * frame_len))
    profile = jnp.sinc(offset) * taper
    profile = profile * jnp.sqrt(frame_len / jnp.sum(profile * profile))
    return profile.reshape(tap_count, frame_len)


def dft_rows(first, span_len, frame_len, chan_count, bank_size):
    spacing = bank_size // chan_count
    row = jnp.arange(2 * chan_count, dtype=jnp.int32)
    chosen = row // 2 * spacing + spacing // 2
    sample = first + jnp.arange(span_len, dtype=jnp.int32)
    phases = chosen[:, None] * sample[None, :] % frame_len
    angles = 2.0 * jnp.pi / frame_len * phases.astype(jnp.float32)
    factor = 1.0 / math.sqrt(frame_len)
    wave = jnp.where(row[:, None] % 2 == 0, jnp.cos(angles), -jnp.sin(angles)) * factor
    return wave.astype(jnp.bfloat16).astype(jnp.float32)


def bank_kernel(steps, chunk, volts_ref, weights_ref, out_ref, products, spectra):
    part = pl.program_id(1)
    rows = weights_ref.shape[0] // TAPS
    weights = weights_ref[...]

    for frame in range(chunk):
        products[part * chunk + frame] = lax.dot_general(
            weights,
            volts_ref[frame],
            (((1,), (1,)), ((), ())),
            preferred_element_type=jnp.float32,
        )

    def add_taps(step, carry):
        total = products[step, 0:rows]
        for tap in range(1, TAPS):
            total = total + products[step + tap, tap * rows : (tap + 1) * rows]
        spectra[pl.ds(step, rows, stride=steps), :] = total
        return carry

    low = jnp.maximum(part * chunk - (TAPS - 1), 0)
    lax.fori_loop(low, (part + 1) * chunk - (TAPS - 1), add_taps, 0)

    @pl.when(part == pl.num_programs(1) - 1)
    def _():
        out_ref[0] = spectra[...].astype(jnp.bfloat16)


def filter_bank(voltages, weights):
    frames, panel_len, span_len = voltages.shape
    steps = frames - TAPS + 1
    rows = weights.shape[0] // TAPS
    chunk = next(size for size in (41, 3, 1) if frames % size == 0)
    return pl.pallas_call(
        functools.partial(bank_kernel, steps, chunk),
        grid=(panel_len // LANES, frames // chunk),
        in_specs=[
            pl.BlockSpec((chunk, LANES, span_len), lambda s, f: (f, s, 0)),
            pl.BlockSpec(weights.shape, lambda s, f: (0, 0)),
        ],
        out_specs=pl.BlockSpec((1, rows * steps, LANES), lambda s, f: (s, 0, 0)),
        out_shape=jax.ShapeDtypeStruct((panel_len // LANES, rows * steps, LANES), jnp.bfloat16),
        scratch_shapes=[
            pltpu.VMEM((frames, weights.shape[0], LANES), jnp.float32),
            pltpu.VMEM((rows * steps, LANES), jnp.float32),
        ],
        compiler_params=pltpu.CompilerParams(vmem_limit_bytes=48 * 1024 * 1024),
    )(voltages, weights)


def spread_kernel(n, terms_ref, all_ref, own_ref, got_core, half, got_chip, core_sems, chip_sems,
                  ring_send, ring_recv, local_sems):
    sec, ch, blk = lax.axis_index("sec"), lax.axis_index("ch"), lax.axis_index("blk")
    other_sec, other_ch = 1 - sec, 1 - ch
    chunks = terms_ref.shape[0]
    group = own_ref.shape[1]
    hops = n // 2

    def block_at(place):
        place = lax.rem(place + 2 * n, n)
        return 2 * place + place // (n // 2) * (2 * n - 1 - 4 * place)

    place = blk // 2 + lax.rem(blk, 2) * (n - 1 - 2 * (blk // 2))
    sides = (block_at(place + 1), block_at(place - 1))

    barrier = pltpu.get_barrier_semaphore()
    partners = ({"sec": other_sec}, {"ch": other_ch}, {"blk": sides[0]}, {"blk": sides[1]})
    for partner in partners:
        pl.semaphore_signal(barrier, inc=1, device_id=partner, device_id_type=MESH)
    pl.semaphore_wait(barrier, len(partners))

    def core_copy(q):
        return pltpu.make_async_remote_copy(
            src_ref=terms_ref.at[q, pl.ds(other_sec * 2 * group, 2 * group)],
            dst_ref=got_core.at[q],
            send_sem=core_sems.at[0, q],
            recv_sem=core_sems.at[1, q],
            device_id={"sec": other_sec},
            device_id_type=MESH,
        )

    def chip_copy(q):
        return pltpu.make_async_remote_copy(
            src_ref=half.at[q],
            dst_ref=got_chip.at[q],
            send_sem=chip_sems.at[0, q],
            recv_sem=chip_sems.at[1, q],
            device_id={"ch": other_ch},
            device_id_type=MESH,
        )

    def ring_copy(q, side, hop):
        origin = block_at(place - (hop - 1) * (1 - 2 * side))
        source = own_ref.at[q] if hop == 1 else all_ref.at[origin, q]
        target = all_ref.at[origin, q]
        if hop == hops:
            piece = pl.ds(side * (group // 2), group // 2)
            source, target = source.at[piece], target.at[piece]
        return pltpu.make_async_remote_copy(
            src_ref=source,
            dst_ref=target,
            send_sem=ring_send.at[side, hop - 1, q],
            recv_sem=ring_recv.at[side, hop - 1, q],
            device_id={"blk": sides[side]},
            device_id_type=MESH,
        )

    def local_copy(q):
        return pltpu.make_async_copy(own_ref.at[q], all_ref.at[blk, q], local_sems.at[q])

    def pair_sum(q, start):
        mine = terms_ref[q, pl.ds(sec * 2 * group + start, group)].astype(jnp.float32)
        return mine + got_core[q, pl.ds(start, group)].astype(jnp.float32)

    def over_cores(q):
        core_copy(q).wait_recv()
        half[q] = pair_sum(q, other_ch * group).astype(jnp.bfloat16)
        chip_copy(q).start()

    def over_chips(q):
        total = pair_sum(q, ch * group)
        chip_copy(q).wait_recv()
        own_ref[q] = (total + got_chip[q].astype(jnp.float32)).astype(jnp.bfloat16)
        for side in range(2):
            ring_copy(q, side, 1).start()
        local_copy(q).start()

    def forward(q, hop):
        for side in range(2):
            ring_copy(q, side, hop).wait_recv()
            ring_copy(q, side, hop + 1).start()

    events = []
    for q in range(chunks):
        events.append((2 * q, q, over_cores, (q,)))
        events.append((2 * q + 2, q, over_chips, (q,)))
        for hop in range(1, hops):
            events.append((2 * q + 2 + hop, q, forward, (q, hop)))
    for q in range(chunks):
        core_copy(q).start()
    for _, _, act, values in sorted(events, key=lambda event: event[:2]):
        act(*values)
    for q in range(chunks):
        for side in range(2):
            ring_copy(q, side, hops).wait_recv()
    for q in range(chunks):
        core_copy(q).wait_send()
        chip_copy(q).wait_send()
        local_copy(q).wait()
        for side in range(2):
            for hop in range(1, hops + 1):
                ring_copy(q, side, hop).wait_send()


def spread(terms):
    n = lax.axis_size("blk")
    chunks, chans, depth, lanes = terms.shape
    group = chans // (lax.axis_size("sec") * lax.axis_size("ch"))
    piece = (chunks, group, depth, lanes)
    return pl.pallas_call(
        functools.partial(spread_kernel, n),
        in_specs=[pl.BlockSpec(memory_space=pltpu.VMEM)],
        out_specs=[pl.BlockSpec(memory_space=pl.ANY), pl.BlockSpec(memory_space=pltpu.VMEM)],
        out_shape=[
            jax.ShapeDtypeStruct((n,) + piece, jnp.bfloat16),
            jax.ShapeDtypeStruct(piece, jnp.bfloat16),
        ],
        scratch_shapes=[
            pltpu.VMEM((chunks, 2 * group, depth, lanes), jnp.bfloat16),
            pltpu.VMEM(piece, jnp.bfloat16),
            pltpu.VMEM(piece, jnp.bfloat16),
            pltpu.SemaphoreType.DMA((2, chunks)),
            pltpu.SemaphoreType.DMA((2, chunks)),
            pltpu.SemaphoreType.DMA((2, n // 2, chunks)),
            pltpu.SemaphoreType.DMA((2, n // 2, chunks)),
            pltpu.SemaphoreType.DMA((chunks,)),
        ],
        compiler_params=pltpu.CompilerParams(
            collective_id=0, has_side_effects=True, vmem_limit_bytes=48 * 1024 * 1024
        ),
    )(terms)


def pair_kernel(steps, local_ref, remote_ref, out_ref, lhs):
    chunks, lanes = local_ref.shape[0], local_ref.shape[3]
    panel_len = chunks * lanes

    @pl.when(pl.program_id(1) == 0)
    def _():
        for q in range(chunks):
            turned = local_ref[q, 0].astype(jnp.float32).T
            lhs[q * lanes : (q + 1) * lanes, :] = turned.astype(jnp.bfloat16)
            other = jnp.concatenate([turned[:, steps:], -turned[:, :steps]], axis=1)
            low = panel_len + q * lanes
            lhs[low : low + lanes, :] = other.astype(jnp.bfloat16)

    remote = jnp.concatenate([remote_ref[0, q, 0] for q in range(chunks)], axis=1)
    sums = jnp.dot(lhs[...], remote, preferred_element_type=jnp.float32)
    scaled = (sums * (1.0 / steps)).astype(jnp.bfloat16)
    out_ref[0, 0] = scaled[:panel_len]
    out_ref[0, 1] = scaled[panel_len:]


def correlate(local, gathered):
    panels, chunks, chans, depth, lanes = gathered.shape
    panel_len = chunks * lanes
    return pl.pallas_call(
        functools.partial(pair_kernel, depth // 2),
        grid=(chans, panels),
        in_specs=[
            pl.BlockSpec((chunks, 1, depth, lanes), lambda c, j: (0, c, 0, 0)),
            pl.BlockSpec((1, chunks, 1, depth, lanes), lambda c, j: (j, 0, c, 0, 0)),
        ],
        out_specs=pl.BlockSpec((1, 2, panel_len, panel_len), lambda c, j: (c, 0, 0, j)),
        out_shape=jax.ShapeDtypeStruct((chans, 2, panel_len, panels * panel_len), jnp.bfloat16),
        scratch_shapes=[pltpu.VMEM((2 * panel_len, depth), jnp.bfloat16)],
        compiler_params=pltpu.CompilerParams(vmem_limit_bytes=32 * 1024 * 1024),
    )(local, gathered)


def body(voltages):
    groups = lax.axis_size("sec") * lax.axis_size("ch")
    frames, panel_len, span_len = voltages.shape
    steps = frames - TAPS + 1
    chan_total = CH_GRP * groups
    group_pos = lax.axis_index("sec") * lax.axis_size("ch") + lax.axis_index("ch")
    first = group_pos * span_len
    window = lax.dynamic_slice_in_dim(make_window(TAPS, FFT), first, span_len, 1)
    table = dft_rows(first, span_len, FFT, chan_total, FFT // 2)
    weights = (window[:, None, :] * table[None]).astype(jnp.bfloat16)
    terms = filter_bank(voltages, weights.reshape(TAPS * 2 * chan_total, span_len))
    gathered, own = spread(terms.reshape(panel_len // LANES, chan_total, 2 * steps, LANES))
    return correlate(own, gathered)


def solution(mesh):
    return jax.shard_map(
        body,
        mesh=mesh,
        in_specs=(P(None, "blk", ("sec", "ch")),),
        out_specs=P(("sec", "ch"), None, "blk", None),
        check_vma=False,
    )
```

```python
import functools
import math

import jax
import jax.numpy as jnp
from jax import lax
from jax.experimental import pallas as pl
from jax.experimental.pallas import tpu as pltpu
from jax.sharding import PartitionSpec as P

FFT = 2048
TAPS = 4
CH_GRP = 4
LANES = 128
MESH = pl.DeviceIdType.MESH


def make_window(tap_count, frame_len):
    position = jnp.arange(tap_count * frame_len, dtype=jnp.float32)
    offset = (position - tap_count * frame_len / 2 + 0.5) / frame_len
    taper = 0.5 - 0.5 * jnp.cos(2.0 * jnp.pi * (position + 0.5) / (tap_count * frame_len))
    profile = jnp.sinc(offset) * taper
    profile = profile * jnp.sqrt(frame_len / jnp.sum(profile * profile))
    return profile.reshape(tap_count, frame_len)


def dft_rows(first, span_len, frame_len, chan_count, bank_size):
    spacing = bank_size // chan_count
    row = jnp.arange(2 * chan_count, dtype=jnp.int32)
    chosen = row // 2 * spacing + spacing // 2
    sample = first + jnp.arange(span_len, dtype=jnp.int32)
    phases = chosen[:, None] * sample[None, :] % frame_len
    angles = 2.0 * jnp.pi / frame_len * phases.astype(jnp.float32)
    factor = 1.0 / math.sqrt(frame_len)
    wave = jnp.where(row[:, None] % 2 == 0, jnp.cos(angles), -jnp.sin(angles)) * factor
    return wave.astype(jnp.bfloat16).astype(jnp.float32)


def spread_kernel(n, volts_ref, weights_ref, all_ref, own_ref, volts, products, spectra, terms_ref, got_core,
                  half, got_chip, volts_sems, core_sems, chip_sems, ring_send, ring_recv, local_sems):
    sec, ch, blk = lax.axis_index("sec"), lax.axis_index("ch"), lax.axis_index("blk")
    other_sec, other_ch = 1 - sec, 1 - ch
    chunks = terms_ref.shape[0]
    group = own_ref.shape[1]
    hops = n // 2
    frames, part_len = volts_ref.shape[0], volts.shape[1]
    parts, steps = frames // part_len, frames - TAPS + 1
    rows = weights_ref.shape[0] // TAPS

    def block_at(place):
        place = lax.rem(place + 2 * n, n)
        return 2 * place + place // (n // 2) * (2 * n - 1 - 4 * place)

    place = blk // 2 + lax.rem(blk, 2) * (n - 1 - 2 * (blk // 2))
    sides = (block_at(place + 1), block_at(place - 1))

    barrier = pltpu.get_barrier_semaphore()
    partners = ({"sec": other_sec}, {"ch": other_ch}, {"blk": sides[0]}, {"blk": sides[1]})
    for partner in partners:
        pl.semaphore_signal(barrier, inc=1, device_id=partner, device_id_type=MESH)

    def volts_copy(index):
        slot = lax.rem(index, 2)
        return pltpu.make_async_copy(
            volts_ref.at[
                pl.ds(lax.rem(index, parts) * part_len, part_len), pl.ds(index // parts * LANES, LANES)
            ],
            volts.at[slot],
            volts_sems.at[slot],
        )

    def produce(q, extras):
        def one_part(part, carry):
            index = q * parts + part
            slot = lax.rem(index, 2)
            volts_copy(index).wait()

            @pl.when(index + 1 < chunks * parts)
            def _():
                volts_copy(index + 1).start()

            weights = weights_ref[...]
            for frame in range(part_len):
                products[part * part_len + frame] = lax.dot_general(
                    weights,
                    volts[slot, frame],
                    (((1,), (1,)), ((), ())),
                    preferred_element_type=jnp.float32,
                )

            def add_taps(step, carry):
                total = products[step, 0:rows]
                for tap in range(1, TAPS):
                    total = total + products[step + tap, tap * rows : (tap + 1) * rows]
                spectra[pl.ds(step, rows, stride=steps), :] = total
                return carry

            low = jnp.maximum(part * part_len - (TAPS - 1), 0)
            lax.fori_loop(low, (part + 1) * part_len - (TAPS - 1), add_taps, 0)

            for place_in_bank, acts in extras.items():
                @pl.when(part == place_in_bank)
                def _():
                    for act, values in acts:
                        act(*values)

            return carry

        lax.fori_loop(0, parts, one_part, 0)
        terms_ref[q] = spectra[...].reshape(terms_ref.shape[1:]).astype(jnp.bfloat16)

    def core_copy(q):
        return pltpu.make_async_remote_copy(
            src_ref=terms_ref.at[q, pl.ds(other_sec * 2 * group, 2 * group)],
            dst_ref=got_core.at[q],
            send_sem=core_sems.at[0, q],
            recv_sem=core_sems.at[1, q],
            device_id={"sec": other_sec},
            device_id_type=MESH,
        )

    def chip_copy(q):
        return pltpu.make_async_remote_copy(
            src_ref=half.at[q],
            dst_ref=got_chip.at[q],
            send_sem=chip_sems.at[0, q],
            recv_sem=chip_sems.at[1, q],
            device_id={"ch": other_ch},
            device_id_type=MESH,
        )

    def ring_copy(q, side, hop):
        origin = block_at(place - (hop - 1) * (1 - 2 * side))
        source = own_ref.at[q] if hop == 1 else all_ref.at[origin, q]
        target = all_ref.at[origin, q]
        if hop == hops:
            piece = pl.ds(side * (group // 2), group // 2)
            source, target = source.at[piece], target.at[piece]
        return pltpu.make_async_remote_copy(
            src_ref=source,
            dst_ref=target,
            send_sem=ring_send.at[side, hop - 1, q],
            recv_sem=ring_recv.at[side, hop - 1, q],
            device_id={"blk": sides[side]},
            device_id_type=MESH,
        )

    def local_copy(q):
        return pltpu.make_async_copy(own_ref.at[q], all_ref.at[blk, q], local_sems.at[q])

    def pair_sum(q, start):
        mine = terms_ref[q, pl.ds(sec * 2 * group + start, group)].astype(jnp.float32)
        return mine + got_core[q, pl.ds(start, group)].astype(jnp.float32)

    def over_cores(q):
        core_copy(q).wait_recv()
        half[q] = pair_sum(q, other_ch * group).astype(jnp.bfloat16)
        chip_copy(q).start()

    def over_chips(q):
        total = pair_sum(q, ch * group)
        chip_copy(q).wait_recv()
        own_ref[q] = (total + got_chip[q].astype(jnp.float32)).astype(jnp.bfloat16)
        for side in range(2):
            ring_copy(q, side, 1).start()
        local_copy(q).start()

    def forward(q, hop):
        for side in range(2):
            ring_copy(q, side, hop).wait_recv()
            ring_copy(q, side, hop + 1).start()

    events = []
    for q in range(chunks):
        events.append((2 * q - 1, q, over_cores, (q,)))
        events.append((2 * q + 2, q, over_chips, (q,)))
        for hop in range(1, hops):
            events.append((2 * q + 2 + hop, q, forward, (q, hop)))
    events = [event[2:] for event in sorted(events, key=lambda event: event[:2])]

    volts_copy(0).start()
    for q in range(chunks):
        early = [(over_cores, (q - 1,)), (over_chips, (q - 2,)), (forward, (q - 3, 1))]
        late = [(forward, (q - 3, 2))]
        early = [event for event in early if event in events]
        late = [event for event in late if event in events]
        events = [event for event in events if event not in early + late]
        extras = {0: early + late} if parts == 1 else {0: early, parts - 1: late}
        produce(q, {part: acts for part, acts in extras.items() if acts})
        if q == 0:
            pl.semaphore_wait(barrier, len(partners))
        core_copy(q).start()
    for act, values in events:
        act(*values)
    for q in range(chunks):
        for side in range(2):
            ring_copy(q, side, hops).wait_recv()
    for q in range(chunks):
        core_copy(q).wait_send()
        chip_copy(q).wait_send()
        local_copy(q).wait()
        for side in range(2):
            for hop in range(1, hops + 1):
                ring_copy(q, side, hop).wait_send()


def spread(voltages, weights):
    n = lax.axis_size("blk")
    frames, panel_len, span_len = voltages.shape
    steps = frames - TAPS + 1
    rows = weights.shape[0] // TAPS
    chunks, lanes, depth = panel_len // LANES, LANES, 2 * steps
    part_len = next(size for size in (41, 3, 1) if frames % size == 0)
    group = rows // 2 // (lax.axis_size("sec") * lax.axis_size("ch"))
    piece = (chunks, group, depth, lanes)
    return pl.pallas_call(
        functools.partial(spread_kernel, n),
        in_specs=[pl.BlockSpec(memory_space=pl.ANY), pl.BlockSpec(memory_space=pltpu.VMEM)],
        out_specs=[pl.BlockSpec(memory_space=pl.ANY), pl.BlockSpec(memory_space=pltpu.VMEM)],
        out_shape=[
            jax.ShapeDtypeStruct((n,) + piece, jnp.bfloat16),
            jax.ShapeDtypeStruct(piece, jnp.bfloat16),
        ],
        scratch_shapes=[
            pltpu.VMEM((2, part_len, lanes, span_len), jnp.bfloat16),
            pltpu.VMEM((frames, weights.shape[0], lanes), jnp.float32),
            pltpu.VMEM((rows * steps, lanes), jnp.float32),
            pltpu.VMEM((chunks, rows // 2, depth, lanes), jnp.bfloat16),
            pltpu.VMEM((chunks, 2 * group, depth, lanes), jnp.bfloat16),
            pltpu.VMEM(piece, jnp.bfloat16),
            pltpu.VMEM(piece, jnp.bfloat16),
            pltpu.SemaphoreType.DMA((2,)),
            pltpu.SemaphoreType.DMA((2, chunks)),
            pltpu.SemaphoreType.DMA((2, chunks)),
            pltpu.SemaphoreType.DMA((2, n // 2, chunks)),
            pltpu.SemaphoreType.DMA((2, n // 2, chunks)),
            pltpu.SemaphoreType.DMA((chunks,)),
        ],
        compiler_params=pltpu.CompilerParams(
            collective_id=0, has_side_effects=True, vmem_limit_bytes=56 * 1024 * 1024
        ),
    )(voltages, weights)


def pair_kernel(steps, local_ref, remote_ref, out_ref, lhs):
    chunks, lanes = local_ref.shape[0], local_ref.shape[3]
    panel_len = chunks * lanes

    @pl.when(pl.program_id(1) == 0)
    def _():
        for q in range(chunks):
            turned = local_ref[q, 0].astype(jnp.float32).T
            lhs[q * lanes : (q + 1) * lanes, :] = turned.astype(jnp.bfloat16)
            other = jnp.concatenate([turned[:, steps:], -turned[:, :steps]], axis=1)
            low = panel_len + q * lanes
            lhs[low : low + lanes, :] = other.astype(jnp.bfloat16)

    for place in range(remote_ref.shape[0]):
        remote = jnp.concatenate([remote_ref[place, q, 0] for q in range(chunks)], axis=1)
        sums = jnp.dot(lhs[...], remote, preferred_element_type=jnp.float32)
        scaled = (sums * (1.0 / steps)).astype(jnp.bfloat16)
        span = slice(place * panel_len, (place + 1) * panel_len)
        out_ref[0, 0, :, span] = scaled[:panel_len]
        out_ref[0, 1, :, span] = scaled[panel_len:]


def correlate(local, gathered):
    panels, chunks, chans, depth, lanes = gathered.shape
    panel_len = chunks * lanes
    batch = 2 if panels % 2 == 0 else 1
    return pl.pallas_call(
        functools.partial(pair_kernel, depth // 2),
        grid=(chans, panels // batch),
        in_specs=[
            pl.BlockSpec((chunks, 1, depth, lanes), lambda c, j: (0, c, 0, 0)),
            pl.BlockSpec((batch, chunks, 1, depth, lanes), lambda c, j: (j, 0, c, 0, 0)),
        ],
        out_specs=pl.BlockSpec((1, 2, panel_len, batch * panel_len), lambda c, j: (c, 0, 0, j)),
        out_shape=jax.ShapeDtypeStruct((chans, 2, panel_len, panels * panel_len), jnp.bfloat16),
        scratch_shapes=[pltpu.VMEM((2 * panel_len, depth), jnp.bfloat16)],
        compiler_params=pltpu.CompilerParams(vmem_limit_bytes=56 * 1024 * 1024),
    )(local, gathered)


def body(voltages):
    groups = lax.axis_size("sec") * lax.axis_size("ch")
    frames, panel_len, span_len = voltages.shape
    steps = frames - TAPS + 1
    chan_total = CH_GRP * groups
    group_pos = lax.axis_index("sec") * lax.axis_size("ch") + lax.axis_index("ch")
    first = group_pos * span_len
    window = lax.dynamic_slice_in_dim(make_window(TAPS, FFT), first, span_len, 1)
    table = dft_rows(first, span_len, FFT, chan_total, FFT // 2)
    weights = (window[:, None, :] * table[None]).astype(jnp.bfloat16)
    gathered, own = spread(voltages, weights.reshape(TAPS * 2 * chan_total, span_len))
    return correlate(own, gathered)


def solution(mesh):
    return jax.shard_map(
        body,
        mesh=mesh,
        in_specs=(P(None, "blk", ("sec", "ch")),),
        out_specs=P(("sec", "ch"), None, "blk", None),
        check_vma=False,
    )
```

```python
import functools
import math

import jax
import jax.numpy as jnp
from jax import lax
from jax.experimental import pallas as pl
from jax.experimental.pallas import tpu as pltpu
from jax.sharding import PartitionSpec as P

FFT = 2048
TAPS = 4
CH_GRP = 4
LANES = 128
MESH = pl.DeviceIdType.MESH


def make_window(tap_count, frame_len):
    position = jnp.arange(tap_count * frame_len, dtype=jnp.float32)
    offset = (position - tap_count * frame_len / 2 + 0.5) / frame_len
    taper = 0.5 - 0.5 * jnp.cos(2.0 * jnp.pi * (position + 0.5) / (tap_count * frame_len))
    profile = jnp.sinc(offset) * taper
    profile = profile * jnp.sqrt(frame_len / jnp.sum(profile * profile))
    return profile.reshape(tap_count, frame_len)


def dft_rows(first, span_len, frame_len, chan_count, bank_size):
    spacing = bank_size // chan_count
    row = jnp.arange(2 * chan_count, dtype=jnp.int32)
    chosen = row // 2 * spacing + spacing // 2
    sample = first + jnp.arange(span_len, dtype=jnp.int32)
    phases = chosen[:, None] * sample[None, :] % frame_len
    angles = 2.0 * jnp.pi / frame_len * phases.astype(jnp.float32)
    factor = 1.0 / math.sqrt(frame_len)
    wave = jnp.where(row[:, None] % 2 == 0, jnp.cos(angles), -jnp.sin(angles)) * factor
    return wave.astype(jnp.bfloat16).astype(jnp.float32)


def spread_kernel(n, volts_ref, weights_ref, all_ref, own_ref, volts, products, spectra, terms_ref, got_core,
                  half, got_chip, volts_sems, core_sems, chip_sems, ring_send, ring_recv, local_sems):
    sec, ch, blk = lax.axis_index("sec"), lax.axis_index("ch"), lax.axis_index("blk")
    other_sec, other_ch = 1 - sec, 1 - ch
    chunks = terms_ref.shape[0]
    group = own_ref.shape[1]
    hops = n // 2
    frames, part_len = volts_ref.shape[0], volts.shape[1]
    parts, steps = frames // part_len, frames - TAPS + 1
    rows = weights_ref.shape[0] // TAPS

    def block_at(place):
        place = lax.rem(place + 2 * n, n)
        return 2 * place + place // (n // 2) * (2 * n - 1 - 4 * place)

    place = blk // 2 + lax.rem(blk, 2) * (n - 1 - 2 * (blk // 2))
    sides = (block_at(place + 1), block_at(place - 1))

    barrier = pltpu.get_barrier_semaphore()
    partners = ({"sec": other_sec}, {"ch": other_ch}, {"blk": sides[0]}, {"blk": sides[1]})
    for partner in partners:
        pl.semaphore_signal(barrier, inc=1, device_id=partner, device_id_type=MESH)

    def volts_copy(index):
        slot = lax.rem(index, 2)
        return pltpu.make_async_copy(
            volts_ref.at[
                pl.ds(lax.rem(index, parts) * part_len, part_len), pl.ds(index // parts * LANES, LANES)
            ],
            volts.at[slot],
            volts_sems.at[slot],
        )

    def produce(q, extras):
        def one_part(part, carry):
            index = q * parts + part
            slot = lax.rem(index, 2)
            volts_copy(index).wait()

            @pl.when(index + 1 < chunks * parts)
            def _():
                volts_copy(index + 1).start()

            weights = weights_ref[...]
            for frame in range(part_len):
                products[part * part_len + frame] = lax.dot_general(
                    weights,
                    volts[slot, frame],
                    (((1,), (1,)), ((), ())),
                    preferred_element_type=jnp.float32,
                )

            def add_taps(step, carry):
                total = products[step, 0:rows]
                for tap in range(1, TAPS):
                    total = total + products[step + tap, tap * rows : (tap + 1) * rows]
                spectra[pl.ds(step, rows, stride=steps), :] = total
                return carry

            low = jnp.maximum(part * part_len - (TAPS - 1), 0)
            lax.fori_loop(low, (part + 1) * part_len - (TAPS - 1), add_taps, 0)

            for place_in_bank, acts in extras.items():
                @pl.when(part == place_in_bank)
                def _():
                    for act, values in acts:
                        act(*values)

            return carry

        lax.fori_loop(0, parts, one_part, 0)
        terms_ref[q] = spectra[...].reshape(terms_ref.shape[1:]).astype(jnp.bfloat16)

    def core_copy(q):
        return pltpu.make_async_remote_copy(
            src_ref=terms_ref.at[q, pl.ds(other_sec * 2 * group, 2 * group)],
            dst_ref=got_core.at[q],
            send_sem=core_sems.at[0, q],
            recv_sem=core_sems.at[1, q],
            device_id={"sec": other_sec},
            device_id_type=MESH,
        )

    def chip_copy(q):
        return pltpu.make_async_remote_copy(
            src_ref=half.at[q],
            dst_ref=got_chip.at[q],
            send_sem=chip_sems.at[0, q],
            recv_sem=chip_sems.at[1, q],
            device_id={"ch": other_ch},
            device_id_type=MESH,
        )

    def ring_copy(q, side, hop):
        origin = block_at(place - (hop - 1) * (1 - 2 * side))
        source = own_ref.at[q] if hop == 1 else all_ref.at[origin, q]
        target = all_ref.at[origin, q]
        if hop == hops:
            piece = pl.ds(side * (group // 2), group // 2)
            source, target = source.at[piece], target.at[piece]
        return pltpu.make_async_remote_copy(
            src_ref=source,
            dst_ref=target,
            send_sem=ring_send.at[side, hop - 1, q],
            recv_sem=ring_recv.at[side, hop - 1, q],
            device_id={"blk": sides[side]},
            device_id_type=MESH,
        )

    def local_copy(q):
        return pltpu.make_async_copy(own_ref.at[q], all_ref.at[blk, q], local_sems.at[q])

    def pair_sum(q, start):
        mine = terms_ref[q, pl.ds(sec * 2 * group + start, group)].astype(jnp.float32)
        return mine + got_core[q, pl.ds(start, group)].astype(jnp.float32)

    def over_cores(q):
        core_copy(q).wait_recv()
        half[q] = pair_sum(q, other_ch * group).astype(jnp.bfloat16)
        chip_copy(q).start()

    def over_chips(q):
        total = pair_sum(q, ch * group)
        chip_copy(q).wait_recv()
        own_ref[q] = (total + got_chip[q].astype(jnp.float32)).astype(jnp.bfloat16)
        for side in range(2):
            ring_copy(q, side, 1).start()
        local_copy(q).start()

    def forward(q, hop):
        for side in range(2):
            ring_copy(q, side, hop).wait_recv()
            ring_copy(q, side, hop + 1).start()

    events = []
    for q in range(chunks):
        events.append((2 * q - 1, q, over_cores, (q,)))
        events.append((2 * q + 2, q, over_chips, (q,)))
        for hop in range(1, hops):
            events.append((2 * q + 2 + hop, q, forward, (q, hop)))
    events = [event[2:] for event in sorted(events, key=lambda event: event[:2])]

    volts_copy(0).start()
    for q in range(chunks):
        early = [(over_cores, (q - 1,)), (over_chips, (q - 2,)), (forward, (q - 3, 1))]
        late = [(forward, (q - 3, 2))]
        early = [event for event in early if event in events]
        late = [event for event in late if event in events]
        events = [event for event in events if event not in early + late]
        extras = {0: early + late} if parts == 1 else {0: early, parts - 1: late}
        produce(q, {part: acts for part, acts in extras.items() if acts})
        if q == 0:
            pl.semaphore_wait(barrier, len(partners))
        core_copy(q).start()
    for act, values in events:
        act(*values)
    for q in range(chunks):
        for side in range(2):
            ring_copy(q, side, hops).wait_recv()
    for q in range(chunks):
        core_copy(q).wait_send()
        chip_copy(q).wait_send()
        local_copy(q).wait()
        for side in range(2):
            for hop in range(1, hops + 1):
                ring_copy(q, side, hop).wait_send()


def spread(voltages, weights):
    n = lax.axis_size("blk")
    frames, panel_len, span_len = voltages.shape
    steps = frames - TAPS + 1
    rows = weights.shape[0] // TAPS
    chunks, lanes, depth = panel_len // LANES, LANES, 2 * steps
    part_len = next(size for size in (41, 3, 1) if frames % size == 0)
    group = rows // 2 // (lax.axis_size("sec") * lax.axis_size("ch"))
    piece = (chunks, group, depth, lanes)
    return pl.pallas_call(
        functools.partial(spread_kernel, n),
        in_specs=[pl.BlockSpec(memory_space=pl.ANY), pl.BlockSpec(memory_space=pltpu.VMEM)],
        out_specs=[pl.BlockSpec(memory_space=pl.ANY), pl.BlockSpec(memory_space=pltpu.VMEM)],
        out_shape=[
            jax.ShapeDtypeStruct((n,) + piece, jnp.bfloat16),
            jax.ShapeDtypeStruct(piece, jnp.bfloat16),
        ],
        scratch_shapes=[
            pltpu.VMEM((2, part_len, lanes, span_len), jnp.bfloat16),
            pltpu.VMEM((frames, weights.shape[0], lanes), jnp.float32),
            pltpu.VMEM((rows * steps, lanes), jnp.float32),
            pltpu.VMEM((chunks, rows // 2, depth, lanes), jnp.bfloat16),
            pltpu.VMEM((chunks, 2 * group, depth, lanes), jnp.bfloat16),
            pltpu.VMEM(piece, jnp.bfloat16),
            pltpu.VMEM(piece, jnp.bfloat16),
            pltpu.SemaphoreType.DMA((2,)),
            pltpu.SemaphoreType.DMA((2, chunks)),
            pltpu.SemaphoreType.DMA((2, chunks)),
            pltpu.SemaphoreType.DMA((2, n // 2, chunks)),
            pltpu.SemaphoreType.DMA((2, n // 2, chunks)),
            pltpu.SemaphoreType.DMA((chunks,)),
        ],
        compiler_params=pltpu.CompilerParams(
            collective_id=0, has_side_effects=True, vmem_limit_bytes=56 * 1024 * 1024
        ),
    )(voltages, weights)


def pair_kernel(steps, local_ref, remote_ref, out_ref, lhs):
    chunks, lanes = local_ref.shape[0], local_ref.shape[3]
    panel_len = chunks * lanes

    @pl.when(pl.program_id(1) == 0)
    def _():
        for q in range(chunks):
            turned = local_ref[q, 0].astype(jnp.float32).T
            lhs[q * lanes : (q + 1) * lanes, :] = turned.astype(jnp.bfloat16)
            other = jnp.concatenate([turned[:, steps:], -turned[:, :steps]], axis=1)
            low = panel_len + q * lanes
            lhs[low : low + lanes, :] = other.astype(jnp.bfloat16)

    for place in range(remote_ref.shape[0]):
        remote = jnp.concatenate([remote_ref[place, q, 0] for q in range(chunks)], axis=1)
        sums = jnp.dot(lhs[...], remote, preferred_element_type=jnp.float32)
        scaled = (sums * (1.0 / steps)).astype(jnp.bfloat16)
        span = slice(place * panel_len, (place + 1) * panel_len)
        out_ref[0, 0, :, span] = scaled[:panel_len]
        out_ref[0, 1, :, span] = scaled[panel_len:]


def correlate(local, gathered):
    panels, chunks, chans, depth, lanes = gathered.shape
    panel_len = chunks * lanes
    batch = 8 if panels % 8 == 0 else 1
    return pl.pallas_call(
        functools.partial(pair_kernel, depth // 2),
        grid=(chans, panels // batch),
        in_specs=[
            pl.BlockSpec((chunks, 1, depth, lanes), lambda c, j: (0, c, 0, 0)),
            pl.BlockSpec((batch, chunks, 1, depth, lanes), lambda c, j: (j, 0, c, 0, 0)),
        ],
        out_specs=pl.BlockSpec((1, 2, panel_len, batch * panel_len), lambda c, j: (c, 0, 0, j)),
        out_shape=jax.ShapeDtypeStruct((chans, 2, panel_len, panels * panel_len), jnp.bfloat16),
        scratch_shapes=[pltpu.VMEM((2 * panel_len, depth), jnp.bfloat16)],
        compiler_params=pltpu.CompilerParams(vmem_limit_bytes=56 * 1024 * 1024),
    )(local, gathered)


def body(voltages):
    groups = lax.axis_size("sec") * lax.axis_size("ch")
    frames, panel_len, span_len = voltages.shape
    steps = frames - TAPS + 1
    chan_total = CH_GRP * groups
    group_pos = lax.axis_index("sec") * lax.axis_size("ch") + lax.axis_index("ch")
    first = group_pos * span_len
    window = lax.dynamic_slice_in_dim(make_window(TAPS, FFT), first, span_len, 1)
    table = dft_rows(first, span_len, FFT, chan_total, FFT // 2)
    weights = (window[:, None, :] * table[None]).astype(jnp.bfloat16)
    gathered, own = spread(voltages, weights.reshape(TAPS * 2 * chan_total, span_len))
    return correlate(own, gathered)


def solution(mesh):
    return jax.shard_map(
        body,
        mesh=mesh,
        in_specs=(P(None, "blk", ("sec", "ch")),),
        out_specs=P(("sec", "ch"), None, "blk", None),
        check_vma=False,
    )
```
